32 devices in a mesh: fsdp: 4 (over z), tp: 4 (over y, core), sect: 2 (over x).
Axes of the slice: x: 2, y: 2, z: 4, core: 2. Of those that a mesh axis runs over, the one named last changes fastest.
Arguments:
- hidden: bfloat16 [4096, 8192], P('fsdp', 'sect'), may hold values from -6 to 6
- kv_weight: bfloat16 [8192, 2048], P(('sect', 'fsdp'), 'tp'), may hold values from -0.0625 to 0.0625
- readout: float32 [2048], P(('tp', 'sect')), may hold values from -0.125 to 0.125
- lengths: int32 [4, 4], P('fsdp'), may hold values from 1 to 512, as said below
- prompt_mask: int32 [4096], P('fsdp'), may hold values from 0 to 1, as said below
- group_ids: int32 [16], P('fsdp'), may hold values from 0 to 1
Outputs:
- keys_values: bfloat16 [4096, 2048], P('fsdp', ('tp', 'sect'))
- advantages: float32 [16], P('fsdp')
The draws below stay inside these ranges and needn't reach their ends.
Inputs may be any that keep to these rules, and one draw needn't show every extreme that they name: `lengths`: each row sums to 1024; some entry of each row equals 512. `prompt_mask`: within each sequence the zeros come before the ones; at each index of fsdp exactly one sequence has no ones.
All inputs are finite; a program needn't handle non-finite values.
Results may differ from the reference program's by a relative error of at most 0.00045.
Values may be sent and summed in bfloat16 or wider, within the bound.
A program may use at most 64 MiB of HBM per device.

```python
import jax
import jax.numpy as jnp
from jax import lax

D = 8192
KVW = 2048
TOK_DEV = 1024
SEQ_DEV = 4
MOST = 512
TOKENS = 4096
SEQS = 16
GROUPS = 2
N_FSDP = 4


def make_layout(key):
    layout_key = jax.random.fold_in(key, 7321)
    row_keys = jax.random.split(layout_key, N_FSDP)

    def one_row(row_key):
        perm_key, where_key, blank_key, prompt_key = jax.random.split(row_key, 4)
        remain = TOK_DEV - MOST
        cut_points = jnp.sort(jax.random.permutation(perm_key, remain - 1)[:SEQ_DEV - 2] + 1).astype(jnp.int32)
        borders = jnp.concatenate([jnp.zeros((1,), jnp.int32), cut_points, jnp.full((1,), remain, jnp.int32)])
        pieces = borders[1:] - borders[:-1]
        longest = jax.random.randint(where_key, (), 0, SEQ_DEV)
        slot_ids = jnp.arange(SEQ_DEV, dtype=jnp.int32)
        source = jnp.clip(jnp.where(slot_ids < longest, slot_ids, slot_ids - 1), 0, SEQ_DEV - 2)
        row_len = jnp.where(slot_ids == longest, MOST, pieces[source]).astype(jnp.int32)
        blank_seq = (longest + 1 + jax.random.randint(blank_key, (), 0, SEQ_DEV - 1)) % SEQ_DEV
        prompt = jax.random.randint(prompt_key, (SEQ_DEV,), 0, row_len).astype(jnp.int32)
        prompt = jnp.where(slot_ids == blank_seq, row_len, prompt)
        finish = jnp.cumsum(row_len).astype(jnp.int32)
        starts = finish - row_len
        answer = starts + prompt
        places = jnp.arange(TOK_DEV, dtype=jnp.int32)
        inside = (places[None, :] >= answer[:, None]) & (places[None, :] < finish[:, None])
        row_mask = jnp.sum(inside.astype(jnp.int32), axis=0).astype(jnp.int32)
        return (row_len, row_mask)
    all_lengths, all_masks = jax.vmap(one_row)(row_keys)
    return (all_lengths, all_masks.reshape(TOK_DEV * N_FSDP))


def draw_lengths(key, part):
    return make_layout(key)[0]


def draw_prompt_mask(key, part):
    return make_layout(key)[1]


def set_ends(drawn, stream_key, low, high):
    extent = drawn.shape
    spot = [jax.random.randint(jax.random.fold_in(stream_key, axis), (), 0, extent[axis]) for axis in range(len(extent))]
    drawn = drawn.at[tuple(spot)].set(low)
    longest = extent.index(max(extent))
    spot[longest] = (spot[longest] + 1) % extent[longest]
    return drawn.at[tuple(spot)].set(high)


def level_of(rng, extent, cuts, least, largest):
    gain, own = 1.0, jax.random.fold_in(rng, 6)
    for axis_at, parts in cuts:
        heights = jnp.exp(jax.random.uniform(jax.random.fold_in(own, axis_at), (parts,), jnp.float32, least / len(cuts), largest / len(cuts)))
        gain = gain * jnp.repeat(heights, extent[axis_at] // parts).reshape([-1 if axis == axis_at else 1 for axis in range(len(extent))])
    return gain


def bell_draw(rng, extent, spread, limit, cuts=(), kind=jnp.bfloat16):
    level = level_of(rng, extent, cuts, -0.22, 0.18) if cuts else 1.0
    result = jax.random.normal(rng, extent, jnp.float32) * spread * level
    return jnp.minimum(jnp.maximum(result, -limit), limit).astype(kind)


def setup_inputs(seed: int = 0) -> dict:
    splits = jax.random.split(jax.random.key(seed), 7)
    hidden = bell_draw(splits[0], (TOKENS, D), 1.0, 6.0, ((0, 4), (1, 2)))
    kv_weight = bell_draw(splits[1], (D, KVW), D ** -0.5, 0.0625, ((0, 8), (1, 4)))
    readout = bell_draw(splits[2], (KVW,), KVW ** -0.5, 0.125, ((0, 8),), jnp.float32)
    lengths = draw_lengths(jax.random.fold_in(splits[6], 71), 0)
    prompt_mask = draw_prompt_mask(jax.random.fold_in(splits[6], 71), 0)
    group_ids = set_ends(jax.random.randint(splits[5], (SEQS,), 0, GROUPS), jax.random.fold_in(splits[5], 1), 0, GROUPS - 1).astype(jnp.int32)
    return dict(hidden=hidden, kv_weight=kv_weight, readout=readout, lengths=lengths, prompt_mask=prompt_mask, group_ids=group_ids)


def reference(hidden, kv_weight, readout, lengths, prompt_mask, group_ids):
    proj = jnp.dot(hidden, kv_weight, preferred_element_type=jnp.float32)
    keys_values = proj.astype(jnp.bfloat16)
    token_score = jnp.dot(proj, readout, precision=lax.Precision.HIGHEST)
    maskf = prompt_mask.astype(jnp.float32)
    masked = (token_score * maskf).reshape(N_FSDP, TOK_DEV)
    maskr = maskf.reshape(N_FSDP, TOK_DEV)
    ends = jnp.cumsum(lengths, axis=1).astype(jnp.int32)
    starts = ends - lengths
    places = jnp.arange(TOK_DEV, dtype=jnp.int32)
    member = ((places[None, None, :] >= starts[:, :, None]) & (places[None, None, :] < ends[:, :, None])).astype(jnp.float32)
    seq_sum = lax.optimization_barrier(jnp.sum(member * masked[:, None, :], axis=2)).reshape(SEQS)
    count = lax.optimization_barrier(jnp.sum(member * maskr[:, None, :], axis=2)).reshape(SEQS)
    reward = seq_sum / jnp.sqrt(jnp.maximum(count, 1.0))
    onehot = (group_ids[:, None] == jnp.arange(GROUPS, dtype=jnp.int32)[None, :]).astype(jnp.float32)
    sizes = lax.optimization_barrier(jnp.sum(onehot, axis=0))
    mean_g = lax.optimization_barrier(jnp.sum(onehot * reward[:, None], axis=0)) / jnp.maximum(sizes, 1.0)
    mine = lax.optimization_barrier(jnp.sum(onehot * mean_g[None, :], axis=1))
    var_g = lax.optimization_barrier(jnp.sum(onehot * ((reward - mine) ** 2)[:, None], axis=0)) / jnp.maximum(sizes, 1.0)
    myvar = lax.optimization_barrier(jnp.sum(onehot * var_g[None, :], axis=1))
    advantages = (reward - mine) / jnp.sqrt(myvar + 1.0)
    return (keys_values, advantages)
```

```python
import functools

import jax
import jax.numpy as jnp
from jax import lax
from jax.experimental import pallas as pl
from jax.experimental.pallas import tpu as pltpu
from jax.sharding import PartitionSpec as P

MESH = pl.DeviceIdType.MESH


def kernel(
    n, nt, ns, chunks, tile,
    hid_any, w_any, ro_ref, mask_ref, len_ref, gid_ref,
    kv_any, adv_ref,
    hid, wbuf, psend, precv, kvbuf, member, sbuf, zbuf,
    hid_sem, own_sem, kv_sem, wsend, wrecv, xsend, xrecv, ssend, srecv, zsend, zrecv,
):
    f, t, s = lax.axis_index("fsdp"), lax.axis_index("tp"), lax.axis_index("sect")
    plane = nt * ns
    me = t * ns + s
    rows, width = w_any.shape
    cw = width // chunks
    half = chunks // 2
    tok = hid.shape[0]

    def plane_id(k):
        other = lax.rem(me + k, plane)
        return {"tp": lax.div(other, ns), "sect": lax.rem(other, ns)}

    def line_id(k):
        return {"fsdp": lax.rem(f + k, n)}

    def cols(c):
        start = lax.rem(c * cw + (1 - s) * (width // 2), width)
        return pl.ds(pl.multiple_of(start, cw), cw)

    def block(c, j):
        return wbuf.at[c, pl.ds(pl.multiple_of(j * rows, rows), rows), :]

    def w_copy(c, j, step, own):
        return pltpu.make_async_remote_copy(
            src_ref=w_any.at[:, cols(c)] if own else block(c, j),
            dst_ref=block(c, j),
            send_sem=wsend.at[0 if step > 0 else 1, c, j],
            recv_sem=wrecv.at[c, j],
            device_id={"fsdp": f + step},
            device_id_type=MESH,
        )

    def x_copy(c):
        return pltpu.make_async_remote_copy(
            src_ref=psend.at[c],
            dst_ref=precv.at[c],
            send_sem=xsend.at[c],
            recv_sem=xrecv.at[c],
            device_id={"sect": 1 - s},
            device_id_type=MESH,
        )

    def s_copy(k, slot):
        return pltpu.make_async_remote_copy(
            src_ref=sbuf.at[slot],
            dst_ref=sbuf.at[slot],
            send_sem=ssend.at[k],
            recv_sem=srecv.at[slot],
            device_id=plane_id(k),
            device_id_type=MESH,
        )

    def z_copy(k, slot):
        return pltpu.make_async_remote_copy(
            src_ref=zbuf.at[slot],
            dst_ref=zbuf.at[slot],
            send_sem=zsend.at[k],
            recv_sem=zrecv.at[slot],
            device_id=line_id(k),
            device_id_type=MESH,
        )

    def each(low, high, body):
        def step(i, carry):
            body(i)
            return carry

        lax.fori_loop(low, high, step, 0)

    barrier = pltpu.get_barrier_semaphore()
    each(1, n, lambda k: pl.semaphore_signal(
        barrier, inc=1, device_id=line_id(k), device_id_type=MESH))
    each(1, plane, lambda k: pl.semaphore_signal(
        barrier, inc=1, device_id=plane_id(k), device_id_type=MESH))

    def own_copy(c):
        return pltpu.make_async_copy(w_any.at[:, cols(c)], block(c, f), own_sem.at[c])

    pl.semaphore_wait(barrier, n - 1 + plane - 1)

    for c in range(chunks):
        @pl.when(f < n - 1)
        def _():
            w_copy(c, f, 1, True).start()

        @pl.when(f > 0)
        def _():
            w_copy(c, f, -1, True).start()

    hid_copy = pltpu.make_async_copy(hid_any, hid, hid_sem)
    for c in range(chunks):
        own_copy(c).start()
    hid_copy.start()

    place = lax.broadcasted_iota(jnp.int32, (8, tok), 1)
    seq = lax.broadcasted_iota(jnp.int32, (8, tok), 0)
    inside = jnp.zeros((8, tok), jnp.bool_)
    start = jnp.int32(0)
    n_seq = len_ref.shape[1]
    for j in range(n_seq):
        finish = start + len_ref[0, j]
        inside = inside | ((seq == j) & (place >= start) & (place < finish))
        start = finish
    member[...] = inside.astype(jnp.float32) * mask_ref[...].astype(jnp.float32)

    total = jnp.zeros((8, cw), jnp.float32)
    for c in range(chunks):
        def arrive(d, c=c):
            left, right = f - d, f + d

            @pl.when(left >= 0)
            def _():
                w_copy(c, left, -1, False).wait_recv()

                @pl.when(f < n - 1)
                def _():
                    w_copy(c, left, 1, False).start()

            @pl.when(right < n)
            def _():
                w_copy(c, right, 1, False).wait_recv()

                @pl.when(f > 0)
                def _():
                    w_copy(c, right, -1, False).start()

        each(1, n, arrive)
        own_copy(c).wait()
        if c == 0:
            hid_copy.wait()
        if c >= half:
            x_copy(c - half).wait_recv()
        own = c - half

        def product(i, carry, c=c, own=own):
            at = pl.ds(pl.multiple_of(i * tile, tile), tile)
            part = jnp.dot(hid[at, :], wbuf[c], preferred_element_type=jnp.float32)
            if c < half:
                psend[c, at, :] = part
                return carry
            projected = part + precv[own, at, :]
            kvbuf[at, own * cw:(own + 1) * cw] = projected.astype(jnp.bfloat16)
            picked = jnp.dot(
                member[:, at], projected,
                precision=lax.Precision.HIGHEST, preferred_element_type=jnp.float32,
            )
            return carry + picked * ro_ref[:, own * cw:(own + 1) * cw]

        total = lax.fori_loop(0, tok // tile, product, total)
        if c < half:
            x_copy(c).start()

    kv_copy = pltpu.make_async_copy(kvbuf, kv_any, kv_sem)
    kv_copy.start()
    sbuf[me] = total
    each(1, plane, lambda k: s_copy(k, me).start())
    count = jnp.sum(member[...], axis=1, keepdims=True)
    each(1, plane, lambda k: s_copy(k, lax.rem(me + k, plane)).wait_recv())
    seq_sum = jnp.sum(jnp.sum(sbuf[...], axis=0), axis=1, keepdims=True)
    reward = seq_sum / jnp.sqrt(jnp.maximum(count, 1.0))

    row = lax.broadcasted_iota(jnp.int32, (8, 128), 0)
    lane = lax.broadcasted_iota(jnp.int32, (8, 128), 1)
    row_gid = jnp.full((8, 128), -1, jnp.int32)
    lane_gid = jnp.full((8, 128), -2, jnp.int32)
    for j in range(n_seq):
        row_gid = jnp.where(row == j, gid_ref[j], row_gid)
        lane_gid = jnp.where(lane == j, gid_ref[j], lane_gid)
    reward = jnp.broadcast_to(reward, (8, 128))
    zbuf[f, 0] = reward
    zbuf[f, 1] = row_gid.astype(jnp.float32)
    each(1, n, lambda k: z_copy(k, f).start())
    mine = jnp.sum(jnp.where(row == lane, reward, 0.0), axis=0, keepdims=True)
    each(1, n, lambda k: z_copy(k, lax.rem(f + k, n)).wait_recv())
    same = (zbuf[:, 1] == lane_gid.astype(jnp.float32)[None]).astype(jnp.float32)
    rewards = zbuf[:, 0]

    def over(value):
        return jnp.sum(jnp.sum(value, axis=0), axis=0, keepdims=True)

    size = jnp.maximum(over(same), 1.0)
    mean = over(same * rewards) / size
    var = over(same * (rewards - mean[None]) ** 2) / size
    adv_ref[...] = ((mine - mean) / jnp.sqrt(var + 1.0))[:, :n_seq]

    each(1, plane, lambda k: s_copy(k, me).wait_send())
    each(1, n, lambda k: z_copy(k, f).wait_send())
    for c in range(half):
        x_copy(c).wait_send()
    for c in range(chunks):
        def sent(j, c=c):
            @pl.when((j <= f) & (f < n - 1))
            def _():
                w_copy(c, j, 1, False).wait_send()

            @pl.when((j >= f) & (f > 0))
            def _():
                w_copy(c, j, -1, False).wait_send()

        each(0, n, sent)
    kv_copy.wait()


def solution(mesh):
    n, nt, ns = mesh.shape["fsdp"], mesh.shape["tp"], mesh.shape["sect"]

    def local(hidden, kv_weight, readout, lengths, prompt_mask, group_ids):
        tok, depth = hidden.shape
        rows, width = kv_weight.shape
        chunks = 4 if n <= 16 else 2
        cw = width // chunks
        half = chunks // 2
        plane = nt * ns
        n_seq = lengths.shape[1]
        dma = pltpu.SemaphoreType.DMA
        vmem, smem, anywhere = (
            pl.BlockSpec(memory_space=pltpu.VMEM),
            pl.BlockSpec(memory_space=pltpu.SMEM),
            pl.BlockSpec(memory_space=pl.ANY),
        )
        kv, adv = pl.pallas_call(
            functools.partial(kernel, n, nt, ns, chunks, min(256, tok)),
            out_shape=(
                jax.ShapeDtypeStruct((tok, width // 2), jnp.bfloat16),
                jax.ShapeDtypeStruct((1, n_seq), jnp.float32),
            ),
            in_specs=[anywhere, anywhere, vmem, vmem, smem, smem],
            out_specs=(anywhere, vmem),
            scratch_shapes=[
                pltpu.VMEM((tok, depth), jnp.bfloat16),
                pltpu.VMEM((chunks, depth, cw), jnp.bfloat16),
                pltpu.VMEM((half, tok, cw), jnp.float32),
                pltpu.VMEM((half, tok, cw), jnp.float32),
                pltpu.VMEM((tok, width // 2), jnp.bfloat16),
                pltpu.VMEM((8, tok), jnp.float32),
                pltpu.VMEM((plane, 8, cw), jnp.float32),
                pltpu.VMEM((n, 2, 8, 128), jnp.float32),
                dma, dma((chunks,)), dma,
                dma((2, chunks, n)), dma((chunks, n)),
                dma((half,)), dma((half,)),
                dma((plane,)), dma((plane,)),
                dma((n,)), dma((n,)),
            ],
            compiler_params=pltpu.CompilerParams(collective_id=0, has_side_effects=True),
        )(hidden, kv_weight, readout[None, :], prompt_mask[None, :], lengths, group_ids)
        return kv, adv[0]

    return jax.shard_map(
        local,
        mesh=mesh,
        in_specs=(
            P("fsdp", "sect"),
            P(("sect", "fsdp"), "tp"),
            P(("tp", "sect")),
            P("fsdp", None),
            P("fsdp"),
            P("fsdp"),
        ),
        out_specs=(P("fsdp", ("tp", "sect")), P("fsdp")),
        check_vma=False,
    )
```

```python
import functools

import jax
import jax.numpy as jnp
from jax import lax
from jax.experimental import pallas as pl
from jax.experimental.pallas import tpu as pltpu
from jax.sharding import PartitionSpec as P

MESH = pl.DeviceIdType.MESH


def kernel(
    n, nt, ns, parts, tile,
    hid_any, w_any, ro_ref, mask_ref, len_ref, gid_ref,
    kv_ref, adv_ref,
    hid, wbuf, acc, precv, member, sbuf, zbuf,
    hid_sem, own_sem, wsend, wrecv, xsend, xrecv, ssend, srecv, zsend, zrecv,
):
    f, t, s = lax.axis_index("fsdp"), lax.axis_index("tp"), lax.axis_index("sect")
    plane = nt * ns
    me = t * ns + s
    rows, width = w_any.shape
    cw = width // 2
    piece = rows // parts
    by_piece = piece % 128 == 0
    tok = hid.shape[0]

    def plane_id(k):
        other = lax.rem(me + k, plane)
        return {"tp": lax.div(other, ns), "sect": lax.rem(other, ns)}

    def line_id(k):
        return {"fsdp": lax.rem(f + k, n)}

    def cols(c):
        side = s if c else 1 - s
        return pl.ds(pl.multiple_of(side * cw, cw), cw)

    def depth_at(j, r):
        return pl.ds(pl.multiple_of(j * rows + r * piece, piece), piece)

    def own_rows(c, r):
        return w_any.at[r * piece:(r + 1) * piece, cols(c)]

    def w_copy(c, j, r, step, own):
        place = wbuf.at[c, depth_at(j, r), :]
        return pltpu.make_async_remote_copy(
            src_ref=own_rows(c, r) if own else place,
            dst_ref=place,
            send_sem=wsend.at[0 if step > 0 else 1, c, r, j],
            recv_sem=wrecv.at[c, r, j],
            device_id={"fsdp": f + step},
            device_id_type=MESH,
        )

    def x_copy():
        return pltpu.make_async_remote_copy(
            src_ref=acc.at[0],
            dst_ref=precv,
            send_sem=xsend,
            recv_sem=xrecv,
            device_id={"sect": 1 - s},
            device_id_type=MESH,
        )

    def s_copy(k, slot):
        return pltpu.make_async_remote_copy(
            src_ref=sbuf.at[slot],
            dst_ref=sbuf.at[slot],
            send_sem=ssend.at[k],
            recv_sem=srecv.at[slot],
            device_id=plane_id(k),
            device_id_type=MESH,
        )

    def z_copy(k, slot):
        return pltpu.make_async_remote_copy(
            src_ref=zbuf.at[slot],
            dst_ref=zbuf.at[slot],
            send_sem=zsend.at[k],
            recv_sem=zrecv.at[slot],
            device_id=line_id(k),
            device_id_type=MESH,
        )

    def each(low, high, body):
        def step(i, carry):
            body(i)
            return carry

        lax.fori_loop(low, high, step, 0)

    barrier = pltpu.get_barrier_semaphore()
    each(1, n, lambda k: pl.semaphore_signal(
        barrier, inc=1, device_id=line_id(k), device_id_type=MESH))
    each(1, plane, lambda k: pl.semaphore_signal(
        barrier, inc=1, device_id=plane_id(k), device_id_type=MESH))

    def own_copy(c, r):
        return pltpu.make_async_copy(
            own_rows(c, r), wbuf.at[c, depth_at(f, r), :], own_sem.at[c, r])

    def send_own(c, step):
        for r in range(parts):
            w_copy(c, f, r, step, True).start()

    pl.semaphore_wait(barrier, n - 1 + plane - 1)

    @pl.when(f < n - 1)
    def _():
        send_own(0, 1)

    @pl.when(f > 0)
    def _():
        send_own(0, -1)

    @pl.when(f == 0)
    def _():
        send_own(1, 1)

    @pl.when(f == n - 1)
    def _():
        send_own(1, -1)

    hid_copy = pltpu.make_async_copy(hid_any, hid, hid_sem)
    for c in range(2):
        for r in range(parts):
            own_copy(c, r).start()
    hid_copy.start()

    place = lax.broadcasted_iota(jnp.int32, (8, tok), 1)
    seq = lax.broadcasted_iota(jnp.int32, (8, tok), 0)
    inside = jnp.zeros((8, tok), jnp.bool_)
    start = jnp.int32(0)
    n_seq = len_ref.shape[1]
    for j in range(n_seq):
        finish = start + len_ref[0, j]
        inside = inside | ((seq == j) & (place >= start) & (place < finish))
        start = finish
    member[...] = inside.astype(jnp.float32) * mask_ref[...].astype(jnp.float32)

    def add(c, depth, first):
        def product(i, carry):
            at = pl.ds(pl.multiple_of(i * tile, tile), tile)
            part = jnp.dot(
                hid[at, depth], wbuf[c, depth, :], preferred_element_type=jnp.float32)
            acc[c, at, :] = part if first else acc[c, at, :] + part
            return carry

        lax.fori_loop(0, tok // tile, product, 0)

    def arrive(c, j, r, step):
        w_copy(c, j, r, -step, False).wait_recv()

        @pl.when((f + step >= 0) & (f + step < n))
        def _():
            w_copy(c, j, r, step, False).start()

        if by_piece:
            add(c, depth_at(j, r), False)

    for c in range(2):
        for r in range(parts):
            own_copy(c, r).wait()
        if c == 0:
            hid_copy.wait()
        if by_piece:
            add(c, pl.ds(pl.multiple_of(f * rows, rows), rows), True)

        def visit(d, c=c):
            left, right = f - d, f + d
            for r in range(parts):
                @pl.when(left >= 0)
                def _():
                    arrive(c, left, r, 1)

                @pl.when(right < n)
                def _():
                    arrive(c, right, r, -1)

            if c == 0:
                @pl.when((d == f) & (f < n - 1))
                def _():
                    send_own(1, 1)

                @pl.when((d == n - 1 - f) & (f > 0))
                def _():
                    send_own(1, -1)

        each(1, n, visit)
        if not by_piece:
            add(c, slice(None), True)
        if c == 0:
            x_copy().start()

    x_copy().wait_recv()

    def finish_rows(i, carry):
        at = pl.ds(pl.multiple_of(i * tile, tile), tile)
        projected = acc[1, at, :] + precv[at, :]
        kv_ref[at, :] = projected.astype(jnp.bfloat16)
        return carry + jnp.dot(
            member[:, at], projected,
            precision=lax.Precision.HIGHEST, preferred_element_type=jnp.float32,
        )

    total = lax.fori_loop(
        0, tok // tile, finish_rows, jnp.zeros((8, cw), jnp.float32)) * ro_ref[...]
    sbuf[me] = total
    each(1, plane, lambda k: s_copy(k, me).start())
    count = jnp.sum(member[...], axis=1, keepdims=True)
    each(1, plane, lambda k: s_copy(k, lax.rem(me + k, plane)).wait_recv())
    seq_sum = jnp.sum(jnp.sum(sbuf[...], axis=0), axis=1, keepdims=True)
    reward = seq_sum / jnp.sqrt(jnp.maximum(count, 1.0))

    row = lax.broadcasted_iota(jnp.int32, (8, 128), 0)
    lane = lax.broadcasted_iota(jnp.int32, (8, 128), 1)
    row_gid = jnp.full((8, 128), -1, jnp.int32)
    lane_gid = jnp.full((8, 128), -2, jnp.int32)
    for j in range(n_seq):
        row_gid = jnp.where(row == j, gid_ref[j], row_gid)
        lane_gid = jnp.where(lane == j, gid_ref[j], lane_gid)
    reward = jnp.broadcast_to(reward, (8, 128))
    zbuf[f, 0] = reward
    zbuf[f, 1] = row_gid.astype(jnp.float32)
    each(1, n, lambda k: z_copy(k, f).start())
    mine = jnp.sum(jnp.where(row == lane, reward, 0.0), axis=0, keepdims=True)
    each(1, n, lambda k: z_copy(k, lax.rem(f + k, n)).wait_recv())
    same = (zbuf[:, 1] == lane_gid.astype(jnp.float32)[None]).astype(jnp.float32)
    rewards = zbuf[:, 0]

    def over(value):
        return jnp.sum(jnp.sum(value, axis=0), axis=0, keepdims=True)

    size = jnp.maximum(over(same), 1.0)
    mean = over(same * rewards) / size
    var = over(same * (rewards - mean[None]) ** 2) / size
    adv_ref[...] = ((mine - mean) / jnp.sqrt(var + 1.0))[:, :n_seq]

    each(1, plane, lambda k: s_copy(k, me).wait_send())
    each(1, n, lambda k: z_copy(k, f).wait_send())
    x_copy().wait_send()
    for c in range(2):
        def sent(j, c=c):
            for r in range(parts):
                @pl.when((j <= f) & (f < n - 1))
                def _():
                    w_copy(c, j, r, 1, False).wait_send()

                @pl.when((j >= f) & (f > 0))
                def _():
                    w_copy(c, j, r, -1, False).wait_send()

        each(0, n, sent)


def solution(mesh):
    n, nt, ns = mesh.shape["fsdp"], mesh.shape["tp"], mesh.shape["sect"]

    def local(hidden, kv_weight, readout, lengths, prompt_mask, group_ids):
        tok, depth = hidden.shape
        rows, width = kv_weight.shape
        parts = max(1, min(2, rows // 256))
        cw = width // 2
        plane = nt * ns
        n_seq = lengths.shape[1]
        dma = pltpu.SemaphoreType.DMA
        vmem, smem, anywhere = (
            pl.BlockSpec(memory_space=pltpu.VMEM),
            pl.BlockSpec(memory_space=pltpu.SMEM),
            pl.BlockSpec(memory_space=pl.ANY),
        )
        kv, adv = pl.pallas_call(
            functools.partial(kernel, n, nt, ns, parts, min(256, tok)),
            out_shape=(
                jax.ShapeDtypeStruct((tok, width // 2), jnp.bfloat16),
                jax.ShapeDtypeStruct((1, n_seq), jnp.float32),
            ),
            in_specs=[anywhere, anywhere, vmem, vmem, smem, smem],
            out_specs=(vmem, vmem),
            scratch_shapes=[
                pltpu.VMEM((tok, depth), jnp.bfloat16),
                pltpu.VMEM((2, depth, cw), jnp.bfloat16),
                pltpu.VMEM((2, tok, cw), jnp.float32),
                pltpu.VMEM((tok, cw), jnp.float32),
                pltpu.VMEM((8, tok), jnp.float32),
                pltpu.VMEM((plane, 8, cw), jnp.float32),
                pltpu.VMEM((n, 2, 8, 128), jnp.float32),
                dma, dma((2, parts)),
                dma((2, 2, parts, n)), dma((2, parts, n)),
                dma, dma,
                dma((plane,)), dma((plane,)),
                dma((n,)), dma((n,)),
            ],
            compiler_params=pltpu.CompilerParams(collective_id=0, has_side_effects=True),
        )(hidden, kv_weight, readout[None, :], prompt_mask[None, :], lengths, group_ids)
        return kv, adv[0]

    return jax.shard_map(
        local,
        mesh=mesh,
        in_specs=(
            P("fsdp", "sect"),
            P(("sect", "fsdp"), "tp"),
            P(("tp", "sect")),
            P("fsdp", None),
            P("fsdp"),
            P("fsdp"),
        ),
        out_specs=(P("fsdp", ("tp", "sect")), P("fsdp")),
        check_vma=False,
    )
```

```python
import functools

import jax
import jax.numpy as jnp
from jax import lax
from jax.experimental import pallas as pl
from jax.experimental.pallas import tpu as pltpu
from jax.sharding import PartitionSpec as P

MESH = pl.DeviceIdType.MESH


def kernel(
    n, nt, ns, parts, tile,
    hid_any, w_any, ro_ref, mask_ref, len_ref, gid_ref,
    kv_ref, adv_ref,
    hid, wbuf, acc, precv, member, sbuf, zbuf,
    hid_sem, own_sem, wsend, wrecv, xsend, xrecv, ssend, srecv, zsend, zrecv,
):
    f, t, s = lax.axis_index("fsdp"), lax.axis_index("tp"), lax.axis_index("sect")
    plane = nt * ns
    me = t * ns + s
    rows, width = w_any.shape
    cw = width // 2
    piece = rows // parts
    by_piece = piece % 128 == 0
    tok = hid.shape[0]

    def plane_id(k):
        other = lax.rem(me + k, plane)
        return {"tp": lax.div(other, ns), "sect": lax.rem(other, ns)}

    def line_id(k):
        return {"fsdp": lax.rem(f + k, n)}

    def cols(c):
        side = s if c else 1 - s
        return pl.ds(pl.multiple_of(side * cw, cw), cw)

    def depth_at(j, r):
        return pl.ds(pl.multiple_of(j * rows + r * piece, piece), piece)

    def own_rows(c, r):
        return w_any.at[r * piece:(r + 1) * piece, cols(c)]

    def w_copy(c, j, r, step, own):
        place = wbuf.at[c, depth_at(j, r), :]
        return pltpu.make_async_remote_copy(
            src_ref=own_rows(c, r) if own else place,
            dst_ref=place,
            send_sem=wsend.at[0 if step > 0 else 1, c, r, j],
            recv_sem=wrecv.at[c, r, j],
            device_id={"fsdp": f + step},
            device_id_type=MESH,
        )

    def x_copy():
        return pltpu.make_async_remote_copy(
            src_ref=acc.at[0],
            dst_ref=precv,
            send_sem=xsend,
            recv_sem=xrecv,
            device_id={"sect": 1 - s},
            device_id_type=MESH,
        )

    def s_copy(k, slot):
        return pltpu.make_async_remote_copy(
            src_ref=sbuf.at[slot],
            dst_ref=sbuf.at[slot],
            send_sem=ssend.at[k],
            recv_sem=srecv.at[slot],
            device_id=plane_id(k),
            device_id_type=MESH,
        )

    def z_copy(k, slot):
        return pltpu.make_async_remote_copy(
            src_ref=zbuf.at[slot],
            dst_ref=zbuf.at[slot],
            send_sem=zsend.at[k],
            recv_sem=zrecv.at[slot],
            device_id=line_id(k),
            device_id_type=MESH,
        )

    def each(low, high, body):
        def step(i, carry):
            body(i)
            return carry

        lax.fori_loop(low, high, step, 0)

    barrier = pltpu.get_barrier_semaphore()
    each(1, n, lambda k: pl.semaphore_signal(
        barrier, inc=1, device_id=line_id(k), device_id_type=MESH))
    each(1, plane, lambda k: pl.semaphore_signal(
        barrier, inc=1, device_id=plane_id(k), device_id_type=MESH))

    def own_copy(c, r):
        return pltpu.make_async_copy(
            own_rows(c, r), wbuf.at[c, depth_at(f, r), :], own_sem.at[c, r])

    def send_own(c, step):
        for r in range(parts):
            w_copy(c, f, r, step, True).start()

    pl.semaphore_wait(barrier, n - 1 + plane - 1)

    @pl.when(f < n - 1)
    def _():
        send_own(0, 1)

    @pl.when(f > 0)
    def _():
        send_own(0, -1)

    @pl.when(f == 0)
    def _():
        send_own(1, 1)

    @pl.when(f == n - 1)
    def _():
        send_own(1, -1)

    hid_copy = pltpu.make_async_copy(hid_any, hid, hid_sem)
    for c in range(2):
        for r in range(parts):
            own_copy(c, r).start()
    hid_copy.start()

    place = lax.broadcasted_iota(jnp.int32, (8, tok), 1)
    seq = lax.broadcasted_iota(jnp.int32, (8, tok), 0)
    inside = jnp.zeros((8, tok), jnp.bool_)
    start = jnp.int32(0)
    n_seq = len_ref.shape[1]
    for j in range(n_seq):
        finish = start + len_ref[0, j]
        inside = inside | ((seq == j) & (place >= start) & (place < finish))
        start = finish
    member[...] = inside.astype(jnp.float32) * mask_ref[...].astype(jnp.float32)

    def add(c, depth, first):
        def product(i, carry):
            at = pl.ds(pl.multiple_of(i * tile, tile), tile)
            part = jnp.dot(
                hid[at, depth], wbuf[c, depth, :], preferred_element_type=jnp.float32)
            acc[c, at, :] = part if first else acc[c, at, :] + part
            return carry

        lax.fori_loop(0, tok // tile, product, 0)

    def arrive(c, j, r, step):
        w_copy(c, j, r, -step, False).wait_recv()

        @pl.when((f + step >= 0) & (f + step < n))
        def _():
            w_copy(c, j, r, step, False).start()

        if by_piece:
            add(c, depth_at(j, r), False)

    for c in range(2):
        for r in range(parts):
            own_copy(c, r).wait()
        if c == 0:
            hid_copy.wait()
        if by_piece:
            add(c, pl.ds(pl.multiple_of(f * rows, rows), rows), True)

        def visit(d, c=c):
            left, right = f - d, f + d
            for r in range(parts):
                @pl.when(left >= 0)
                def _():
                    arrive(c, left, r, 1)

                @pl.when(right < n)
                def _():
                    arrive(c, right, r, -1)

            if c == 0:
                @pl.when((d == f) & (f < n - 1))
                def _():
                    send_own(1, 1)

                @pl.when((d == n - 1 - f) & (f > 0))
                def _():
                    send_own(1, -1)

        each(1, n, visit)
        if not by_piece:
            add(c, slice(None), True)
        if c == 0:
            x_copy().start()

    x_copy().wait_recv()

    def finish_rows(i, carry):
        at = pl.ds(pl.multiple_of(i * tile, tile), tile)
        projected = acc[1, at, :] + precv[at, :]
        kv_ref[at, :] = projected.astype(jnp.bfloat16)
        return carry + jnp.dot(
            member[:, at], projected,
            precision=lax.Precision.HIGHEST, preferred_element_type=jnp.float32,
        )

    total = lax.fori_loop(
        0, tok // tile, finish_rows, jnp.zeros((8, cw), jnp.float32)) * ro_ref[...]
    sbuf[me] = total
    each(1, plane, lambda k: s_copy(k, me).start())
    count = jnp.sum(member[...], axis=1, keepdims=True)
    each(1, plane, lambda k: s_copy(k, lax.rem(me + k, plane)).wait_recv())
    seq_sum = jnp.sum(jnp.sum(sbuf[...], axis=0), axis=1, keepdims=True)
    reward = seq_sum / jnp.sqrt(jnp.maximum(count, 1.0))

    row = lax.broadcasted_iota(jnp.int32, (8, 128), 0)
    lane = lax.broadcasted_iota(jnp.int32, (8, 128), 1)
    row_gid = jnp.full((8, 128), -1, jnp.int32)
    lane_gid = jnp.full((8, 128), -2, jnp.int32)
    for j in range(n_seq):
        row_gid = jnp.where(row == j, gid_ref[j], row_gid)
        lane_gid = jnp.where(lane == j, gid_ref[j], lane_gid)
    reward = jnp.broadcast_to(reward, (8, 128))
    zbuf[f, 0] = reward
    zbuf[f, 1] = row_gid.astype(jnp.float32)
    each(1, n, lambda k: z_copy(k, f).start())
    mine = jnp.sum(jnp.where(row == lane, reward, 0.0), axis=0, keepdims=True)
    each(1, n, lambda k: z_copy(k, lax.rem(f + k, n)).wait_recv())
    same = (zbuf[:, 1] == lane_gid.astype(jnp.float32)[None]).astype(jnp.float32)
    rewards = zbuf[:, 0]

    def over(value):
        return jnp.sum(jnp.sum(value, axis=0), axis=0, keepdims=True)

    size = jnp.maximum(over(same), 1.0)
    mean = over(same * rewards) / size
    var = over(same * (rewards - mean[None]) ** 2) / size
    adv_ref[...] = ((mine - mean) / jnp.sqrt(var + 1.0))[:, :n_seq]

    each(1, plane, lambda k: s_copy(k, me).wait_send())
    each(1, n, lambda k: z_copy(k, f).wait_send())
    x_copy().wait_send()
    for c in range(2):
        def sent(j, c=c):
            for r in range(parts):
                @pl.when((j <= f) & (f < n - 1))
                def _():
                    w_copy(c, j, r, 1, False).wait_send()

                @pl.when((j >= f) & (f > 0))
                def _():
                    w_copy(c, j, r, -1, False).wait_send()

        each(0, n, sent)


def hand_over(pieces, kv_any, adv_in, kv_out, adv_out, held, in_sem, out_sem):
    size = held.shape[1]

    def load(i):
        return pltpu.make_async_copy(
            kv_any.at[i * size:(i + 1) * size], held.at[i], in_sem.at[i])

    def store(i):
        return pltpu.make_async_copy(
            held.at[i], kv_out.at[i * size:(i + 1) * size], out_sem.at[i])

    for i in range(pieces):
        load(i).start()
    adv_out[...] = adv_in[...]
    for i in range(pieces):
        load(i).wait()
        store(i).start()
    for i in range(pieces):
        store(i).wait()


def solution(mesh):
    n, nt, ns = mesh.shape["fsdp"], mesh.shape["tp"], mesh.shape["sect"]

    def local(hidden, kv_weight, readout, lengths, prompt_mask, group_ids):
        tok, depth = hidden.shape
        rows, width = kv_weight.shape
        parts = max(1, min(2, rows // 256))
        cw = width // 2
        plane = nt * ns
        n_seq = lengths.shape[1]
        dma = pltpu.SemaphoreType.DMA
        vmem, smem, anywhere = (
            pl.BlockSpec(memory_space=pltpu.VMEM),
            pl.BlockSpec(memory_space=pltpu.SMEM),
            pl.BlockSpec(memory_space=pl.ANY),
        )
        kv, adv = pl.pallas_call(
            functools.partial(kernel, n, nt, ns, parts, min(256, tok)),
            out_shape=(
                jax.ShapeDtypeStruct((tok, width // 2), jnp.bfloat16),
                jax.ShapeDtypeStruct((1, n_seq), jnp.float32),
            ),
            in_specs=[anywhere, anywhere, vmem, vmem, smem, smem],
            out_specs=(vmem, vmem),
            scratch_shapes=[
                pltpu.VMEM((tok, depth), jnp.bfloat16),
                pltpu.VMEM((2, depth, cw), jnp.bfloat16),
                pltpu.VMEM((2, tok, cw), jnp.float32),
                pltpu.VMEM((tok, cw), jnp.float32),
                pltpu.VMEM((8, tok), jnp.float32),
                pltpu.VMEM((plane, 8, cw), jnp.float32),
                pltpu.VMEM((n, 2, 8, 128), jnp.float32),
                dma, dma((2, parts)),
                dma((2, 2, parts, n)), dma((2, parts, n)),
                dma, dma,
                dma((plane,)), dma((plane,)),
                dma((n,)), dma((n,)),
            ],
            compiler_params=pltpu.CompilerParams(collective_id=0, has_side_effects=True),
        )(hidden, kv_weight, readout[None, :], prompt_mask[None, :], lengths, group_ids)
        pieces = 4 if tok % 64 == 0 else 1
        kv, adv = pl.pallas_call(
            functools.partial(hand_over, pieces),
            out_shape=(
                jax.ShapeDtypeStruct((tok, width // 2), jnp.bfloat16),
                jax.ShapeDtypeStruct((1, n_seq), jnp.float32),
            ),
            in_specs=[anywhere, vmem],
            out_specs=(anywhere, vmem),
            scratch_shapes=[
                pltpu.VMEM((pieces, tok // pieces, width // 2), jnp.bfloat16),
                dma((pieces,)),
                dma((pieces,)),
            ],
        )(kv, adv)
        return kv, adv[0]

    return jax.shard_map(
        local,
        mesh=mesh,
        in_specs=(
            P("fsdp", "sect"),
            P(("sect", "fsdp"), "tp"),
            P(("tp", "sect")),
            P("fsdp", None),
            P("fsdp"),
            P("fsdp"),
        ),
        out_specs=(P("fsdp", ("tp", "sect")), P("fsdp")),
        check_vma=False,
    )
```

```python
import functools

import jax
import jax.numpy as jnp
from jax import lax
from jax.experimental import pallas as pl
from jax.experimental.pallas import tpu as pltpu
from jax.sharding import PartitionSpec as P

MESH = pl.DeviceIdType.MESH


def kernel(
    n, nt, ns, parts, tile,
    hid_any, w_any, ro_ref, mask_ref, len_ref, gid_ref,
    kv_ref, adv_ref,
    hid, wbuf, acc, precv, member, sbuf, zbuf,
    hid_sem, own_sem, wsend, wrecv, xsend, xrecv, ssend, srecv, zsend, zrecv,
):
    f, t, s = lax.axis_index("fsdp"), lax.axis_index("tp"), lax.axis_index("sect")
    plane = nt * ns
    me = t * ns + s
    rows, width = w_any.shape
    cw = width // 2
    piece = rows // parts
    by_piece = piece % 128 == 0
    tok = hid.shape[0]

    def plane_id(k):
        other = lax.rem(me + k, plane)
        return {"tp": lax.div(other, ns), "sect": lax.rem(other, ns)}

    def line_id(k):
        return {"fsdp": lax.rem(f + k, n)}

    def cols(c):
        side = s if c else 1 - s
        return pl.ds(pl.multiple_of(side * cw, cw), cw)

    def depth_at(j, r):
        return pl.ds(pl.multiple_of(j * rows + r * piece, piece), piece)

    def own_rows(c, r):
        return w_any.at[r * piece:(r + 1) * piece, cols(c)]

    def w_copy(c, j, r, step, own):
        place = wbuf.at[c, depth_at(j, r), :]
        return pltpu.make_async_remote_copy(
            src_ref=own_rows(c, r) if own else place,
            dst_ref=place,
            send_sem=wsend.at[0 if step > 0 else 1, c, r, j],
            recv_sem=wrecv.at[c, r, j],
            device_id={"fsdp": f + step},
            device_id_type=MESH,
        )

    def x_copy():
        return pltpu.make_async_remote_copy(
            src_ref=acc.at[0],
            dst_ref=precv,
            send_sem=xsend,
            recv_sem=xrecv,
            device_id={"sect": 1 - s},
            device_id_type=MESH,
        )

    def s_copy(k, slot):
        return pltpu.make_async_remote_copy(
            src_ref=sbuf.at[slot],
            dst_ref=sbuf.at[slot],
            send_sem=ssend.at[k],
            recv_sem=srecv.at[slot],
            device_id=plane_id(k),
            device_id_type=MESH,
        )

    def z_copy(k, slot):
        return pltpu.make_async_remote_copy(
            src_ref=zbuf.at[slot],
            dst_ref=zbuf.at[slot],
            send_sem=zsend.at[k],
            recv_sem=zrecv.at[slot],
            device_id=line_id(k),
            device_id_type=MESH,
        )

    def each(low, high, body):
        def step(i, carry):
            body(i)
            return carry

        lax.fori_loop(low, high, step, 0)

    barrier = pltpu.get_barrier_semaphore()
    each(1, n, lambda k: pl.semaphore_signal(
        barrier, inc=1, device_id=line_id(k), device_id_type=MESH))
    each(1, plane, lambda k: pl.semaphore_signal(
        barrier, inc=1, device_id=plane_id(k), device_id_type=MESH))

    def own_copy(c, r):
        return pltpu.make_async_copy(
            own_rows(c, r), wbuf.at[c, depth_at(f, r), :], own_sem.at[c, r])

    def send_own(c, step):
        for r in range(parts):
            w_copy(c, f, r, step, True).start()

    pl.semaphore_wait(barrier, n - 1 + plane - 1)

    @pl.when(f < n - 1)
    def _():
        send_own(0, 1)

    @pl.when(f > 0)
    def _():
        send_own(0, -1)

    @pl.when(f == 0)
    def _():
        send_own(1, 1)

    @pl.when(f == n - 1)
    def _():
        send_own(1, -1)

    hid_copy = pltpu.make_async_copy(hid_any, hid, hid_sem)
    for c in range(2):
        for r in range(parts):
            own_copy(c, r).start()
    hid_copy.start()

    place = lax.broadcasted_iota(jnp.int32, (8, tok), 1)
    seq = lax.broadcasted_iota(jnp.int32, (8, tok), 0)
    inside = jnp.zeros((8, tok), jnp.bool_)
    start = jnp.int32(0)
    n_seq = len_ref.shape[1]
    for j in range(n_seq):
        finish = start + len_ref[0, j]
        inside = inside | ((seq == j) & (place >= start) & (place < finish))
        start = finish
    member[...] = inside.astype(jnp.float32) * mask_ref[...].astype(jnp.float32)

    def add(c, depth, first):
        def product(i, carry):
            at = pl.ds(pl.multiple_of(i * tile, tile), tile)
            part = jnp.dot(
                hid[at, depth], wbuf[c, depth, :], preferred_element_type=jnp.float32)
            acc[c, at, :] = part if first else acc[c, at, :] + part
            return carry

        lax.fori_loop(0, tok // tile, product, 0)

    def arrive(c, j, r, step):
        w_copy(c, j, r, -step, False).wait_recv()

        @pl.when((f + step >= 0) & (f + step < n))
        def _():
            w_copy(c, j, r, step, False).start()

        if by_piece:
            add(c, depth_at(j, r), False)

    for c in range(2):
        for r in range(parts):
            own_copy(c, r).wait()
        if c == 0:
            hid_copy.wait()
        if by_piece:
            add(c, pl.ds(pl.multiple_of(f * rows, rows), rows), True)

        def visit(d, c=c):
            left, right = f - d, f + d
            for r in range(parts):
                @pl.when(left >= 0)
                def _():
                    arrive(c, left, r, 1)

                @pl.when(right < n)
                def _():
                    arrive(c, right, r, -1)

            if c == 0:
                @pl.when((d == f) & (f < n - 1))
                def _():
                    send_own(1, 1)

                @pl.when((d == n - 1 - f) & (f > 0))
                def _():
                    send_own(1, -1)

        each(1, n, visit)
        if not by_piece:
            add(c, slice(None), True)
        if c == 0:
            x_copy().start()

    x_copy().wait_recv()

    def finish_rows(i, carry):
        at = pl.ds(pl.multiple_of(i * tile, tile), tile)
        projected = acc[1, at, :] + precv[at, :]
        kv_ref[at, :] = projected.astype(jnp.bfloat16)
        return carry + jnp.dot(
            member[:, at], projected,
            precision=lax.Precision.HIGHEST, preferred_element_type=jnp.float32,
        )

    total = lax.fori_loop(
        0, tok // tile, finish_rows, jnp.zeros((8, cw), jnp.float32)) * ro_ref[...]
    sbuf[me] = total
    each(1, plane, lambda k: s_copy(k, me).start())
    count = jnp.sum(member[...], axis=1, keepdims=True)
    each(1, plane, lambda k: s_copy(k, lax.rem(me + k, plane)).wait_recv())
    seq_sum = jnp.sum(jnp.sum(sbuf[...], axis=0), axis=1, keepdims=True)
    reward = seq_sum / jnp.sqrt(jnp.maximum(count, 1.0))

    row = lax.broadcasted_iota(jnp.int32, (8, 128), 0)
    lane = lax.broadcasted_iota(jnp.int32, (8, 128), 1)
    row_gid = jnp.full((8, 128), -1, jnp.int32)
    lane_gid = jnp.full((8, 128), -2, jnp.int32)
    for j in range(n_seq):
        row_gid = jnp.where(row == j, gid_ref[j], row_gid)
        lane_gid = jnp.where(lane == j, gid_ref[j], lane_gid)
    reward = jnp.broadcast_to(reward, (8, 128))
    zbuf[f, 0] = reward
    zbuf[f, 1] = row_gid.astype(jnp.float32)
    each(1, n, lambda k: z_copy(k, f).start())
    mine = jnp.sum(jnp.where(row == lane, reward, 0.0), axis=0, keepdims=True)
    each(1, n, lambda k: z_copy(k, lax.rem(f + k, n)).wait_recv())
    same = (zbuf[:, 1] == lane_gid.astype(jnp.float32)[None]).astype(jnp.float32)
    rewards = zbuf[:, 0]

    def over(value):
        return jnp.sum(jnp.sum(value, axis=0), axis=0, keepdims=True)

    size = jnp.maximum(over(same), 1.0)
    mean = over(same * rewards) / size
    var = over(same * (rewards - mean[None]) ** 2) / size
    adv_ref[...] = ((mine - mean) / jnp.sqrt(var + 1.0))[:, :n_seq]

    each(1, plane, lambda k: s_copy(k, me).wait_send())
    each(1, n, lambda k: z_copy(k, f).wait_send())
    x_copy().wait_send()
    for c in range(2):
        def sent(j, c=c):
            for r in range(parts):
                @pl.when((j <= f) & (f < n - 1))
                def _():
                    w_copy(c, j, r, 1, False).wait_send()

                @pl.when((j >= f) & (f > 0))
                def _():
                    w_copy(c, j, r, -1, False).wait_send()

        each(0, n, sent)


def solution(mesh):
    n, nt, ns = mesh.shape["fsdp"], mesh.shape["tp"], mesh.shape["sect"]

    def local(hidden, kv_weight, readout, lengths, prompt_mask, group_ids):
        tok, depth = hidden.shape
        rows, width = kv_weight.shape
        parts = max(1, min(2, rows // 256))
        cw = width // 2
        plane = nt * ns
        n_seq = lengths.shape[1]
        dma = pltpu.SemaphoreType.DMA
        vmem, smem, anywhere = (
            pl.BlockSpec(memory_space=pltpu.VMEM),
            pl.BlockSpec(memory_space=pltpu.SMEM),
            pl.BlockSpec(memory_space=pl.ANY),
        )
        kv, adv = pl.pallas_call(
            functools.partial(kernel, n, nt, ns, parts, min(256, tok)),
            out_shape=(
                pltpu.VMEM((tok, width // 2), jnp.bfloat16),
                pltpu.VMEM((1, n_seq), jnp.float32),
            ),
            in_specs=[anywhere, anywhere, vmem, vmem, smem, smem],
            out_specs=(vmem, vmem),
            scratch_shapes=[
                pltpu.VMEM((tok, depth), jnp.bfloat16),
                pltpu.VMEM((2, depth, cw), jnp.bfloat16),
                pltpu.VMEM((2, tok, cw), jnp.float32),
                pltpu.VMEM((tok, cw), jnp.float32),
                pltpu.VMEM((8, tok), jnp.float32),
                pltpu.VMEM((plane, 8, cw), jnp.float32),
                pltpu.VMEM((n, 2, 8, 128), jnp.float32),
                dma, dma((2, parts)),
                dma((2, 2, parts, n)), dma((2, parts, n)),
                dma, dma,
                dma((plane,)), dma((plane,)),
                dma((n,)), dma((n,)),
            ],
            compiler_params=pltpu.CompilerParams(collective_id=0, has_side_effects=True),
        )(hidden, kv_weight, readout[None, :], prompt_mask[None, :], lengths, group_ids)
        return kv, adv[0]

    return jax.shard_map(
        local,
        mesh=mesh,
        in_specs=(
            P("fsdp", "sect"),
            P(("sect", "fsdp"), "tp"),
            P(("tp", "sect")),
            P("fsdp", None),
            P("fsdp"),
            P("fsdp"),
        ),
        out_specs=(P("fsdp", ("tp", "sect")), P("fsdp")),
        check_vma=False,
    )
```

```python
import functools

import jax
import jax.numpy as jnp
from jax import lax
from jax.experimental import pallas as pl
from jax.experimental.pallas import tpu as pltpu
from jax.sharding import PartitionSpec as P

MESH = pl.DeviceIdType.MESH


def kernel(
    n, nt, ns, parts, tile,
    hid_any, w_any, ro_ref, mask_ref, len_ref, gid_ref,
    kv_ref, adv_ref,
    hid, wbuf, acc, precv, member, sbuf, zbuf,
    hid_sem, own_sem, wsend, wrecv, xsend, xrecv, ssend, srecv, zsend, zrecv,
):
    f, t, s = lax.axis_index("fsdp"), lax.axis_index("tp"), lax.axis_index("sect")
    plane = nt * ns
    me = t * ns + s
    rows, width = w_any.shape
    cw = width // 2
    piece = rows // parts
    by_piece = piece % 128 == 0
    tok = hid.shape[0]

    def plane_id(k):
        other = lax.rem(me + k, plane)
        return {"tp": lax.div(other, ns), "sect": lax.rem(other, ns)}

    def line_id(k):
        return {"fsdp": lax.rem(f + k, n)}

    def cols(c):
        side = s if c else 1 - s
        return pl.ds(pl.multiple_of(side * cw, cw), cw)

    def depth_at(j, r):
        return pl.ds(pl.multiple_of(j * rows + r * piece, piece), piece)

    def own_rows(c, r):
        return w_any.at[r * piece:(r + 1) * piece, cols(c)]

    def w_copy(c, j, r, step, own):
        place = wbuf.at[c, depth_at(j, r), :]
        return pltpu.make_async_remote_copy(
            src_ref=own_rows(c, r) if own else place,
            dst_ref=place,
            send_sem=wsend.at[0 if step > 0 else 1, c, r, j],
            recv_sem=wrecv.at[c, r, j],
            device_id={"fsdp": f + step},
            device_id_type=MESH,
        )

    def x_copy():
        return pltpu.make_async_remote_copy(
            src_ref=acc.at[0],
            dst_ref=precv,
            send_sem=xsend,
            recv_sem=xrecv,
            device_id={"sect": 1 - s},
            device_id_type=MESH,
        )

    def s_copy(k, slot):
        return pltpu.make_async_remote_copy(
            src_ref=sbuf.at[slot],
            dst_ref=sbuf.at[slot],
            send_sem=ssend.at[k],
            recv_sem=srecv.at[slot],
            device_id=plane_id(k),
            device_id_type=MESH,
        )

    def z_copy(k, slot):
        return pltpu.make_async_remote_copy(
            src_ref=zbuf.at[slot],
            dst_ref=zbuf.at[slot],
            send_sem=zsend.at[k],
            recv_sem=zrecv.at[slot],
            device_id=line_id(k),
            device_id_type=MESH,
        )

    def each(low, high, body):
        def step(i, carry):
            body(i)
            return carry

        lax.fori_loop(low, high, step, 0)

    barrier = pltpu.get_barrier_semaphore()
    each(1, n, lambda k: pl.semaphore_signal(
        barrier, inc=1, device_id=line_id(k), device_id_type=MESH))
    each(1, plane, lambda k: pl.semaphore_signal(
        barrier, inc=1, device_id=plane_id(k), device_id_type=MESH))

    def own_copy(c, r):
        return pltpu.make_async_copy(
            own_rows(c, r), wbuf.at[c, depth_at(f, r), :], own_sem.at[c, r])

    def send_own(c, step):
        for r in range(parts):
            w_copy(c, f, r, step, True).start()

    pl.semaphore_wait(barrier, n - 1 + plane - 1)

    @pl.when(f < n - 1)
    def _():
        send_own(0, 1)

    @pl.when(f > 0)
    def _():
        send_own(0, -1)

    @pl.when(f == 0)
    def _():
        send_own(1, 1)

    @pl.when(f == n - 1)
    def _():
        send_own(1, -1)

    hid_copy = pltpu.make_async_copy(hid_any, hid, hid_sem)
    for c in range(2):
        for r in range(parts):
            own_copy(c, r).start()
    hid_copy.start()

    place = lax.broadcasted_iota(jnp.int32, (8, tok), 1)
    seq = lax.broadcasted_iota(jnp.int32, (8, tok), 0)
    inside = jnp.zeros((8, tok), jnp.bool_)
    start = jnp.int32(0)
    n_seq = len_ref.shape[1]
    for j in range(n_seq):
        finish = start + len_ref[0, j]
        inside = inside | ((seq == j) & (place >= start) & (place < finish))
        start = finish
    member[...] = inside.astype(jnp.float32) * mask_ref[...].astype(jnp.float32)

    def add(c, depth, first):
        def product(i, carry):
            at = pl.ds(pl.multiple_of(i * tile, tile), tile)
            part = jnp.dot(
                hid[at, depth], wbuf[c, depth, :], preferred_element_type=jnp.float32)
            acc[c, at, :] = part if first else acc[c, at, :] + part
            return carry

        lax.fori_loop(0, tok // tile, product, 0)

    def arrive(c, j, r, step):
        w_copy(c, j, r, -step, False).wait_recv()

        @pl.when((f + step >= 0) & (f + step < n))
        def _():
            w_copy(c, j, r, step, False).start()

        if by_piece:
            add(c, depth_at(j, r), False)

    for c in range(2):
        for r in range(parts):
            own_copy(c, r).wait()
        if c == 0:
            hid_copy.wait()
        if by_piece:
            add(c, pl.ds(pl.multiple_of(f * rows, rows), rows), True)

        def visit(d, c=c):
            left, right = f - d, f + d
            for r in range(parts):
                @pl.when(left >= 0)
                def _():
                    arrive(c, left, r, 1)

                @pl.when(right < n)
                def _():
                    arrive(c, right, r, -1)

            if c == 0:
                @pl.when((d == f) & (f < n - 1))
                def _():
                    send_own(1, 1)

                @pl.when((d == n - 1 - f) & (f > 0))
                def _():
                    send_own(1, -1)

        each(1, n, visit)
        if not by_piece:
            add(c, slice(None), True)
        if c == 0:
            x_copy().start()

    x_copy().wait_recv()

    def finish_rows(i, carry):
        at = pl.ds(pl.multiple_of(i * tile, tile), tile)
        projected = acc[1, at, :] + precv[at, :]
        kv_ref[at, :] = projected.astype(jnp.bfloat16)
        return carry + jnp.dot(
            member[:, at], projected,
            precision=lax.Precision.HIGHEST, preferred_element_type=jnp.float32,
        )

    total = lax.fori_loop(
        0, tok // tile, finish_rows, jnp.zeros((8, cw), jnp.float32)) * ro_ref[...]
    sbuf[me] = sum(total[:, at:at + 128] for at in range(0, cw, 128))
    each(1, plane, lambda k: s_copy(k, me).start())
    count = jnp.sum(member[...], axis=1, keepdims=True)
    each(1, plane, lambda k: s_copy(k, lax.rem(me + k, plane)).wait_recv())
    seq_sum = jnp.sum(jnp.sum(sbuf[...], axis=0), axis=1, keepdims=True)
    reward = seq_sum / jnp.sqrt(jnp.maximum(count, 1.0))

    row = lax.broadcasted_iota(jnp.int32, (8, 128), 0)
    lane = lax.broadcasted_iota(jnp.int32, (8, 128), 1)
    row_gid = jnp.full((8, 128), -1, jnp.int32)
    lane_gid = jnp.full((8, 128), -2, jnp.int32)
    for j in range(n_seq):
        row_gid = jnp.where(row == j, gid_ref[j], row_gid)
        lane_gid = jnp.where(lane == j, gid_ref[j], lane_gid)
    reward = jnp.broadcast_to(reward, (8, 128))
    zbuf[f, 0] = reward
    zbuf[f, 1] = row_gid.astype(jnp.float32)
    each(1, n, lambda k: z_copy(k, f).start())
    mine = jnp.sum(jnp.where(row == lane, reward, 0.0), axis=0, keepdims=True)
    each(1, n, lambda k: z_copy(k, lax.rem(f + k, n)).wait_recv())
    same = (zbuf[:, 1] == lane_gid.astype(jnp.float32)[None]).astype(jnp.float32)
    rewards = zbuf[:, 0]

    def over(value):
        return jnp.sum(jnp.sum(value, axis=0), axis=0, keepdims=True)

    size = jnp.maximum(over(same), 1.0)
    mean = over(same * rewards) / size
    var = over(same * (rewards - mean[None]) ** 2) / size
    adv_ref[...] = ((mine - mean) / jnp.sqrt(var + 1.0))[:, :n_seq]

    each(1, plane, lambda k: s_copy(k, me).wait_send())
    each(1, n, lambda k: z_copy(k, f).wait_send())
    x_copy().wait_send()
    for c in range(2):
        def sent(j, c=c):
            for r in range(parts):
                @pl.when((j <= f) & (f < n - 1))
                def _():
                    w_copy(c, j, r, 1, False).wait_send()

                @pl.when((j >= f) & (f > 0))
                def _():
                    w_copy(c, j, r, -1, False).wait_send()

        each(0, n, sent)


def solution(mesh):
    n, nt, ns = mesh.shape["fsdp"], mesh.shape["tp"], mesh.shape["sect"]

    def local(hidden, kv_weight, readout, lengths, prompt_mask, group_ids):
        tok, depth = hidden.shape
        rows, width = kv_weight.shape
        parts = max(1, min(4, rows // 256))
        cw = width // 2
        plane = nt * ns
        n_seq = lengths.shape[1]
        dma = pltpu.SemaphoreType.DMA
        vmem, smem, anywhere = (
            pl.BlockSpec(memory_space=pltpu.VMEM),
            pl.BlockSpec(memory_space=pltpu.SMEM),
            pl.BlockSpec(memory_space=pl.ANY),
        )
        kv, adv = pl.pallas_call(
            functools.partial(kernel, n, nt, ns, parts, min(256, tok)),
            out_shape=(
                pltpu.VMEM((tok, width // 2), jnp.bfloat16),
                pltpu.VMEM((1, n_seq), jnp.float32),
            ),
            in_specs=[anywhere, anywhere, vmem, vmem, smem, smem],
            out_specs=(vmem, vmem),
            scratch_shapes=[
                pltpu.VMEM((tok, depth), jnp.bfloat16),
                pltpu.VMEM((2, depth, cw), jnp.bfloat16),
                pltpu.VMEM((2, tok, cw), jnp.float32),
                pltpu.VMEM((tok, cw), jnp.float32),
                pltpu.VMEM((8, tok), jnp.float32),
                pltpu.VMEM((plane, 8, 128), jnp.float32),
                pltpu.VMEM((n, 2, 8, 128), jnp.float32),
                dma, dma((2, parts)),
                dma((2, 2, parts, n)), dma((2, parts, n)),
                dma, dma,
                dma((plane,)), dma((plane,)),
                dma((n,)), dma((n,)),
            ],
            compiler_params=pltpu.CompilerParams(collective_id=0, has_side_effects=True),
        )(hidden, kv_weight, readout[None, :], prompt_mask[None, :], lengths, group_ids)
        return kv, adv[0]

    return jax.shard_map(
        local,
        mesh=mesh,
        in_specs=(
            P("fsdp", "sect"),
            P(("sect", "fsdp"), "tp"),
            P(("tp", "sect")),
            P("fsdp", None),
            P("fsdp"),
            P("fsdp"),
        ),
        out_specs=(P("fsdp", ("tp", "sect")), P("fsdp")),
        check_vma=False,
    )
```

```python
import functools

import jax
import jax.numpy as jnp
from jax import lax
from jax.experimental import pallas as pl
from jax.experimental.pallas import tpu as pltpu
from jax.sharding import PartitionSpec as P

MESH = pl.DeviceIdType.MESH


def kernel(
    n, nt, ns, parts, tile,
    hid_any, w_any, ro_ref, mask_ref, len_ref, gid_ref,
    kv_ref, adv_ref,
    hid, wbuf, acc, precv, member, sbuf, zbuf,
    hid_sem, own_sem, wsend, wrecv, xsend, xrecv, ssend, srecv, zsend, zrecv,
):
    f, t, s = lax.axis_index("fsdp"), lax.axis_index("tp"), lax.axis_index("sect")
    plane = nt * ns
    me = t * ns + s
    rows, width = w_any.shape
    cw = width // 2
    piece = rows // parts
    by_piece = piece % 128 == 0
    tok = hid.shape[0]

    def plane_id(k):
        other = lax.rem(me + k, plane)
        return {"tp": lax.div(other, ns), "sect": lax.rem(other, ns)}

    def line_id(k):
        return {"fsdp": lax.rem(f + k, n)}

    def cols(c):
        side = s if c else 1 - s
        return pl.ds(pl.multiple_of(side * cw, cw), cw)

    def depth_at(j, r):
        return pl.ds(pl.multiple_of(j * rows + r * piece, piece), piece)

    def own_rows(c, r):
        return w_any.at[r * piece:(r + 1) * piece, cols(c)]

    def w_copy(c, j, r, step, own):
        place = wbuf.at[c, depth_at(j, r), :]
        return pltpu.make_async_remote_copy(
            src_ref=own_rows(c, r) if own else place,
            dst_ref=place,
            send_sem=wsend.at[0 if step > 0 else 1, c, r, j],
            recv_sem=wrecv.at[c, r, j],
            device_id={"fsdp": f + step},
            device_id_type=MESH,
        )

    def x_copy():
        return pltpu.make_async_remote_copy(
            src_ref=acc.at[0],
            dst_ref=precv,
            send_sem=xsend,
            recv_sem=xrecv,
            device_id={"sect": 1 - s},
            device_id_type=MESH,
        )

    def s_copy(k, slot):
        return pltpu.make_async_remote_copy(
            src_ref=sbuf.at[slot],
            dst_ref=sbuf.at[slot],
            send_sem=ssend.at[k],
            recv_sem=srecv.at[slot],
            device_id=plane_id(k),
            device_id_type=MESH,
        )

    def z_copy(k, slot):
        return pltpu.make_async_remote_copy(
            src_ref=zbuf.at[slot],
            dst_ref=zbuf.at[slot],
            send_sem=zsend.at[k],
            recv_sem=zrecv.at[slot],
            device_id=line_id(k),
            device_id_type=MESH,
        )

    def each(low, high, body):
        def step(i, carry):
            body(i)
            return carry

        lax.fori_loop(low, high, step, 0)

    barrier = pltpu.get_barrier_semaphore()
    each(1, n, lambda k: pl.semaphore_signal(
        barrier, inc=1, device_id=line_id(k), device_id_type=MESH))
    each(1, plane, lambda k: pl.semaphore_signal(
        barrier, inc=1, device_id=plane_id(k), device_id_type=MESH))

    def own_copy(c, r):
        return pltpu.make_async_copy(
            own_rows(c, r), wbuf.at[c, depth_at(f, r), :], own_sem.at[c, r])

    def send_own(c, step):
        for r in range(parts):
            w_copy(c, f, r, step, True).start()

    pl.semaphore_wait(barrier, n - 1 + plane - 1)

    @pl.when(f < n - 1)
    def _():
        send_own(0, 1)

    @pl.when(f > 0)
    def _():
        send_own(0, -1)

    @pl.when(f == 0)
    def _():
        send_own(1, 1)

    @pl.when(f == n - 1)
    def _():
        send_own(1, -1)

    hid_copy = pltpu.make_async_copy(hid_any, hid, hid_sem)
    for c in range(2):
        for r in range(parts):
            own_copy(c, r).start()
    hid_copy.start()

    place = lax.broadcasted_iota(jnp.int32, (8, tok), 1)
    seq = lax.broadcasted_iota(jnp.int32, (8, tok), 0)
    inside = jnp.zeros((8, tok), jnp.bool_)
    start = jnp.int32(0)
    n_seq = len_ref.shape[1]
    for j in range(n_seq):
        finish = start + len_ref[0, j]
        inside = inside | ((seq == j) & (place >= start) & (place < finish))
        start = finish
    member[...] = inside.astype(jnp.float32) * mask_ref[...].astype(jnp.float32)

    def add(c, depth, first):
        def product(i, carry):
            at = pl.ds(pl.multiple_of(i * tile, tile), tile)
            part = jnp.dot(
                hid[at, depth], wbuf[c, depth, :], preferred_element_type=jnp.float32)
            acc[c, at, :] = part if first else acc[c, at, :] + part
            return carry

        lax.fori_loop(0, tok // tile, product, 0)

    def arrive(c, j, r, step):
        w_copy(c, j, r, -step, False).wait_recv()

        @pl.when((f + step >= 0) & (f + step < n))
        def _():
            w_copy(c, j, r, step, False).start()

        if by_piece:
            add(c, depth_at(j, r), False)

    for c in range(2):
        for r in range(parts):
            own_copy(c, r).wait()
        if c == 0:
            hid_copy.wait()
        if by_piece:
            add(c, pl.ds(pl.multiple_of(f * rows, rows), rows), True)

        def visit(d, c=c):
            left, right = f - d, f + d
            for r in range(parts):
                @pl.when(left >= 0)
                def _():
                    arrive(c, left, r, 1)

                @pl.when(right < n)
                def _():
                    arrive(c, right, r, -1)

            if c == 0:
                @pl.when((d == f) & (f < n - 1))
                def _():
                    send_own(1, 1)

                @pl.when((d == n - 1 - f) & (f > 0))
                def _():
                    send_own(1, -1)

        each(1, n, visit)
        if not by_piece:
            add(c, slice(None), True)
        if c == 0:
            x_copy().start()

    x_copy().wait_recv()

    def finish_rows(i, carry):
        at = pl.ds(pl.multiple_of(i * tile, tile), tile)
        projected = acc[1, at, :] + precv[at, :]
        kv_ref[at, :] = projected.astype(jnp.bfloat16)
        chosen = member[:, at].astype(jnp.bfloat16)
        rest = projected
        for _ in range(3):
            digits = rest.astype(jnp.bfloat16)
            carry += jnp.dot(chosen, digits, preferred_element_type=jnp.float32)
            rest = rest - digits.astype(jnp.float32)
        return carry

    total = lax.fori_loop(
        0, tok // tile, finish_rows, jnp.zeros((8, cw), jnp.float32)) * ro_ref[...]
    sbuf[me] = total
    each(1, plane, lambda k: s_copy(k, me).start())
    count = jnp.sum(member[...], axis=1, keepdims=True)
    each(1, plane, lambda k: s_copy(k, lax.rem(me + k, plane)).wait_recv())
    seq_sum = jnp.sum(jnp.sum(sbuf[...], axis=0), axis=1, keepdims=True)
    reward = seq_sum / jnp.sqrt(jnp.maximum(count, 1.0))

    row = lax.broadcasted_iota(jnp.int32, (8, 128), 0)
    lane = lax.broadcasted_iota(jnp.int32, (8, 128), 1)
    row_gid = jnp.full((8, 128), -1, jnp.int32)
    lane_gid = jnp.full((8, 128), -2, jnp.int32)
    for j in range(n_seq):
        row_gid = jnp.where(row == j, gid_ref[j], row_gid)
        lane_gid = jnp.where(lane == j, gid_ref[j], lane_gid)
    reward = jnp.broadcast_to(reward, (8, 128))
    zbuf[f, 0] = reward
    zbuf[f, 1] = row_gid.astype(jnp.float32)
    each(1, n, lambda k: z_copy(k, f).start())
    mine = jnp.sum(jnp.where(row == lane, reward, 0.0), axis=0, keepdims=True)
    each(1, n, lambda k: z_copy(k, lax.rem(f + k, n)).wait_recv())
    same = (zbuf[:, 1] == lane_gid.astype(jnp.float32)[None]).astype(jnp.float32)
    rewards = zbuf[:, 0]

    def over(value):
        return jnp.sum(jnp.sum(value, axis=0), axis=0, keepdims=True)

    size = jnp.maximum(over(same), 1.0)
    mean = over(same * rewards) / size
    var = over(same * (rewards - mean[None]) ** 2) / size
    adv_ref[...] = ((mine - mean) / jnp.sqrt(var + 1.0))[:, :n_seq]

    each(1, plane, lambda k: s_copy(k, me).wait_send())
    each(1, n, lambda k: z_copy(k, f).wait_send())
    x_copy().wait_send()
    for c in range(2):
        def sent(j, c=c):
            for r in range(parts):
                @pl.when((j <= f) & (f < n - 1))
                def _():
                    w_copy(c, j, r, 1, False).wait_send()

                @pl.when((j >= f) & (f > 0))
                def _():
                    w_copy(c, j, r, -1, False).wait_send()

        each(0, n, sent)


def solution(mesh):
    n, nt, ns = mesh.shape["fsdp"], mesh.shape["tp"], mesh.shape["sect"]

    def local(hidden, kv_weight, readout, lengths, prompt_mask, group_ids):
        tok, depth = hidden.shape
        rows, width = kv_weight.shape
        parts = max(1, min(2, rows // 256))
        cw = width // 2
        plane = nt * ns
        n_seq = lengths.shape[1]
        dma = pltpu.SemaphoreType.DMA
        vmem, smem, anywhere = (
            pl.BlockSpec(memory_space=pltpu.VMEM),
            pl.BlockSpec(memory_space=pltpu.SMEM),
            pl.BlockSpec(memory_space=pl.ANY),
        )
        kv, adv = pl.pallas_call(
            functools.partial(kernel, n, nt, ns, parts, min(256, tok)),
            out_shape=(
                pltpu.VMEM((tok, width // 2), jnp.bfloat16),
                pltpu.VMEM((1, n_seq), jnp.float32),
            ),
            in_specs=[anywhere, anywhere, vmem, vmem, smem, smem],
            out_specs=(vmem, vmem),
            scratch_shapes=[
                pltpu.VMEM((tok, depth), jnp.bfloat16),
                pltpu.VMEM((2, depth, cw), jnp.bfloat16),
                pltpu.VMEM((2, tok, cw), jnp.float32),
                pltpu.VMEM((tok, cw), jnp.float32),
                pltpu.VMEM((8, tok), jnp.float32),
                pltpu.VMEM((plane, 8, cw), jnp.float32),
                pltpu.VMEM((n, 2, 8, 128), jnp.float32),
                dma, dma((2, parts)),
                dma((2, 2, parts, n)), dma((2, parts, n)),
                dma, dma,
                dma((plane,)), dma((plane,)),
                dma((n,)), dma((n,)),
            ],
            compiler_params=pltpu.CompilerParams(collective_id=0, has_side_effects=True),
        )(hidden, kv_weight, readout[None, :], prompt_mask[None, :], lengths, group_ids)
        return kv, adv[0]

    return jax.shard_map(
        local,
        mesh=mesh,
        in_specs=(
            P("fsdp", "sect"),
            P(("sect", "fsdp"), "tp"),
            P(("tp", "sect")),
            P("fsdp", None),
            P("fsdp"),
            P("fsdp"),
        ),
        out_specs=(P("fsdp", ("tp", "sect")), P("fsdp")),
        check_vma=False,
    )
```
